32 devices in a mesh: dp: 16 (over z, y, core), shard: 2 (over x).
Axes of the slice: x: 2, y: 2, z: 4, core: 2. Of those that a mesh axis runs over, the one named last changes fastest.
Arguments:
- tokens: float32 [16384, 1024], P(('dp', 'shard')), may hold values from -6 to 6
- out_grad: float32 [16384, 1024], P(('dp', 'shard')), may hold values from -30 to 30
- segment_ids: int32 [16, 1024], P('dp'), may hold values from 0 to 3, never falling along the last dimension, each value on 1 to 512 neighbouring positions
- qkv_weight: float32 [1024, 3072], P('dp', 'shard'), may hold values from -0.1875 to 0.1875
- proj_weight: float32 [1024, 1024], P('dp', 'shard'), may hold values from -1.5 to 1.5
- up_weight: float32 [1024, 4096], P('dp', 'shard'), may hold values from -0.1875 to 0.1875
- down_weight: float32 [4096, 1024], P('dp', 'shard'), may hold values from -0.09375 to 0.09375
- vectors: float32 [12, 1024], P(None, ('dp', 'shard')), may hold values from -4 to 4
- qkv_moments: float32 [2, 1024, 3072], P(None, 'dp', 'shard'), may hold values from -0.05 to 0.05
- proj_moments: float32 [2, 1024, 1024], P(None, 'dp', 'shard'), may hold values from -0.05 to 0.05
- up_moments: float32 [2, 1024, 4096], P(None, 'dp', 'shard'), may hold values from -0.05 to 0.05
- down_moments: float32 [2, 4096, 1024], P(None, 'dp', 'shard'), may hold values from -0.05 to 0.05
- vector_moments: float32 [2, 12, 1024], P(None, None, ('dp', 'shard')), may hold values from -1 to 1
Outputs:
- block_out: float32 [16384, 1024], P(('dp', 'shard'))
- tokens_grad: float32 [16384, 1024], P(('dp', 'shard'))
- qkv_grad: float32 [1024, 3072], P('dp', 'shard')
- proj_grad: float32 [1024, 1024], P('dp', 'shard')
- up_grad: float32 [1024, 4096], P('dp', 'shard')
- down_grad: float32 [4096, 1024], P('dp', 'shard')
- vectors_grad: float32 [12, 1024], P(None, ('dp', 'shard'))
- qkv_new: float32 [1024, 3072], P('dp', 'shard')
- proj_new: float32 [1024, 1024], P('dp', 'shard')
- up_new: float32 [1024, 4096], P('dp', 'shard')
- down_new: float32 [4096, 1024], P('dp', 'shard')
- vectors_new: float32 [12, 1024], P(None, ('dp', 'shard'))
- qkv_moments_new: float32 [2, 1024, 3072], P(None, 'dp', 'shard')
- proj_moments_new: float32 [2, 1024, 1024], P(None, 'dp', 'shard')
- up_moments_new: float32 [2, 1024, 4096], P(None, 'dp', 'shard')
- down_moments_new: float32 [2, 4096, 1024], P(None, 'dp', 'shard')
- vector_moments_new: float32 [2, 12, 1024], P(None, None, ('dp', 'shard'))
The draws below stay inside these ranges and needn't reach their ends.
All inputs are finite; a program needn't handle non-finite values.
Results may differ from the reference program's by a relative error of at most 0.011.
Values may be sent and summed in bfloat16 or wider, within the bound.
A program may use at most 320 MiB of HBM per device.

```python
import math
import jax
import jax.numpy as jnp
import numpy as np
from jax import lax

D = 1024
FF = 4096
HD = 64
ROT = 16
SEQ_LEN = 1024
DOCS = 4
STEP = 4
VROWS = 12
NPARAM = 12595200
SEQS = 16
TOKENS = 16384


def moment_pair(key, shape):
    first_key = jax.random.fold_in(key, 11)
    second_key = jax.random.fold_in(key, 12)
    first_moment = 0.01 * jax.random.truncated_normal(first_key, -4.0, 4.0, shape, jnp.float32)
    exponent_draw = jax.random.uniform(second_key, shape, jnp.float32, math.log(1e-05), math.log(0.001))
    return jnp.stack([first_moment, jnp.exp(exponent_draw)])


def draw_qkv_moments(key, part):
    return moment_pair(key, (D, 3 * D))


def draw_proj_moments(key, part):
    return moment_pair(key, (D, D))


def draw_up_moments(key, part):
    return moment_pair(key, (D, FF))


def draw_down_moments(key, part):
    return moment_pair(key, (FF, D))


def draw_vector_moments(key, part):
    sign_key = jax.random.fold_in(key, 41)
    size_key = jax.random.fold_in(key, 42)
    second_key = jax.random.fold_in(key, 43)
    shape = (VROWS, D)
    size_log = jax.random.uniform(size_key, shape, jnp.float32, math.log(0.01), math.log(1.0))
    second_log = jax.random.uniform(second_key, shape, jnp.float32, math.log(0.001), math.log(0.5))
    signs = jnp.where(jax.random.uniform(sign_key, shape, jnp.float32) < 0.5, -1.0, 1.0)
    return jnp.stack([signs * jnp.exp(size_log), jnp.exp(second_log)])


def draw_vectors(key, part):
    gain_key = jax.random.fold_in(key, 21)
    bias_key = jax.random.fold_in(key, 22)
    trend_key = jax.random.fold_in(key, 23)
    gains = jax.random.uniform(gain_key, (2, D), jnp.float32, 0.6, 1.4)
    noise_rows = 0.3 * jax.random.truncated_normal(bias_key, -4.0, 4.0, (6, D), jnp.float32)
    trend_noise = 0.5 * jax.random.truncated_normal(trend_key, -3.0, 3.0, (FF,), jnp.float32)
    ramp = -1.0 + 3.0 * jnp.arange(FF, dtype=jnp.float32) / FF
    up_rows = (ramp + trend_noise).reshape(FF // D, D)
    return jnp.concatenate([gains[0:1], noise_rows[0:1], gains[1:2], noise_rows[1:2], noise_rows[2:6], up_rows], axis=0)


def draw_out_grad(key, part):
    base_key = jax.random.fold_in(key, 31)
    row_key = jax.random.fold_in(key, 32)
    column_key = jax.random.fold_in(key, 33)
    column_pos = jnp.arange(D, dtype=jnp.float32) / D
    column_scale = jnp.exp(math.log(10.0) * (column_pos - 0.5)) * jnp.exp(jax.random.uniform(column_key, (D,), jnp.float32, -0.35, 0.35))
    row_scale = jnp.exp(jax.random.uniform(row_key, (TOKENS, 1), jnp.float32, math.log(0.5), math.log(2.0)))
    base_values = jax.random.truncated_normal(base_key, -3.0, 3.0, (TOKENS, D), jnp.float32)
    return base_values * row_scale * column_scale[None, :]


def block_scale(key, extent, cuts, low, top_value):
    factor_of = 1.0
    for dim, shards_of in cuts:
        steps = jax.random.uniform(jax.random.fold_in(jax.random.fold_in(key, 6), dim), (shards_of,), jnp.float32, low / len(cuts), top_value / len(cuts))
        factor_of = factor_of * jnp.repeat(jnp.exp(steps), extent[dim] // shards_of).reshape((-1,) + (1,) * (len(extent) - 1 - dim))
    return factor_of


def split_up(amount, total, limit, lean):
    portions = [(1 << 20) // math.isqrt(standing ** lean) + 1 for standing in range(2, amount + 1)]
    surplus, holding = total - limit - (amount - 1), [1] * (amount - 1)
    while surplus > 0:
        candidates = [i for i in range(amount - 1) if holding[i] < limit]
        whole, budget = sum([portions[i] for i in candidates]), surplus
        for i in candidates:
            more = min(limit - holding[i], max(1, budget * portions[i] // whole), surplus)
            holding[i] = holding[i] + more
            surplus = surplus - more
    return np.array([limit] + holding)


def uneven_parts(key, amount, total, limit, lean):
    if amount == 2:
        one = jax.random.randint(key, (), max(1, total - limit), min(limit, total - 1) + 1)
        return jnp.stack([one, total - one])
    tallies = jnp.asarray(split_up(amount, total, limit, lean), jnp.int32)
    twos = (amount - 1) // 2
    donor, sink = tallies[1:1 + 2 * twos:2], tallies[2:2 + 2 * twos:2]
    margin = jnp.minimum(donor - 1, limit - sink)
    moved = jax.random.randint(jax.random.fold_in(key, 1), (twos,), 0, 1 << 20) % (margin + 1)
    tallies = tallies.at[1:1 + 2 * twos:2].set(donor - moved).at[2:2 + 2 * twos:2].set(sink + moved)
    return tallies[jax.random.permutation(jax.random.fold_in(key, 2), amount)]


def normal_values(own_key, dims, width, limit, pieces=(), kind=jnp.bfloat16):
    entries = width * jax.random.normal(own_key, dims, jnp.float32)
    if pieces:
        entries = entries * block_scale(own_key, dims, pieces, -0.22, 0.18)
    return jnp.clip(entries, -limit, limit).astype(kind)


def setup_inputs(seed: int = 0) -> dict:
    key_of = jax.random.split(jax.random.key(seed), 14)
    return {
        "tokens": normal_values(key_of[0], (TOKENS, D), 1.0, 6.0, ((0, 32),), jnp.float32),
        "out_grad": draw_out_grad(jax.random.fold_in(key_of[13], 71), 0),
        "segment_ids": jax.vmap(lambda own: jnp.searchsorted(jnp.cumsum(uneven_parts(own, DOCS, SEQ_LEN, SEQ_LEN // 2, 0)), jnp.arange(SEQ_LEN), side="right"))(jax.random.split(key_of[2], SEQS)).reshape((SEQS, SEQ_LEN)).astype(jnp.int32),
        "qkv_weight": normal_values(key_of[3], (D, 3 * D), D ** -0.5, 0.1875, ((0, 16), (1, 2)), jnp.float32),
        "proj_weight": normal_values(key_of[4], (D, D), (D // 64) ** -0.5, 1.5, ((0, 16), (1, 2)), jnp.float32),
        "up_weight": normal_values(key_of[5], (D, FF), D ** -0.5, 0.1875, ((0, 16), (1, 2)), jnp.float32),
        "down_weight": normal_values(key_of[6], (FF, D), FF ** -0.5, 0.09375, ((0, 16), (1, 2)), jnp.float32),
        "vectors": draw_vectors(jax.random.fold_in(key_of[13], 71), 0),
        "qkv_moments": draw_qkv_moments(jax.random.fold_in(key_of[13], 71), 0),
        "proj_moments": draw_proj_moments(jax.random.fold_in(key_of[13], 71), 0),
        "up_moments": draw_up_moments(jax.random.fold_in(key_of[13], 71), 0),
        "down_moments": draw_down_moments(jax.random.fold_in(key_of[13], 71), 0),
        "vector_moments": draw_vector_moments(jax.random.fold_in(key_of[13], 71), 0),
    }


ln_eps = 1e-05
beta_one = 0.9
beta_two = 0.95
learn_rate = 0.005
decay_rate = 0.01
adam_eps = 1e-08
rope_base = 10000.0

def rounded(values):
    return lax.optimization_barrier(values.astype(jnp.bfloat16))

def as_float(values):
    return values.astype(jnp.float32)

def norm_rows(inputs, gain_row, bias_row):
    center = inputs - lax.optimization_barrier(jnp.mean(inputs, axis=-1, keepdims=True))
    inverse = lax.rsqrt(lax.optimization_barrier(jnp.mean(center * center, axis=-1, keepdims=True)) + ln_eps)
    unit_rows = center * inverse
    return (unit_rows * gain_row + bias_row, unit_rows, inverse)

def norm_back(upstream, unit_rows, inverse, gain_row):
    gain_grad = lax.optimization_barrier(jnp.sum(upstream * unit_rows, axis=0))
    bias_grad = lax.optimization_barrier(jnp.sum(upstream, axis=0))
    scaled_up = upstream * gain_row
    mean_plain = lax.optimization_barrier(jnp.mean(scaled_up, axis=-1, keepdims=True))
    mean_unit = lax.optimization_barrier(jnp.mean(scaled_up * unit_rows, axis=-1, keepdims=True))
    return (inverse * (scaled_up - mean_plain - unit_rows * mean_unit), gain_grad, bias_grad)

def doc_positions(segment_row):
    length_all = segment_row.shape[0]
    indices = jnp.arange(length_all, dtype=jnp.int32)
    starting = jnp.concatenate([jnp.ones((1,), dtype=jnp.bool_), segment_row[1:] != segment_row[:-1]])
    begins = lax.cummax(jnp.where(starting, indices, 0), axis=0)
    return indices - begins

def rotary_tables(positions, rot_dims):
    half_dims = rot_dims // 2
    exponent = jnp.arange(half_dims, dtype=jnp.float32) * (2.0 / rot_dims)
    inverse_freq = jnp.exp(-math.log(rope_base) * exponent)
    angles = positions.astype(jnp.float32)[:, None] * inverse_freq[None, :]
    return (jnp.cos(angles)[:, None, :], jnp.sin(angles)[:, None, :])

def rotate(head_rows, cosine_table, sine_table):
    half_dims = cosine_table.shape[-1]
    lower_half = head_rows[..., :half_dims]
    upper_half = head_rows[..., half_dims:2 * half_dims]
    return jnp.concatenate([lower_half * cosine_table - upper_half * sine_table, upper_half * cosine_table + lower_half * sine_table, head_rows[..., 2 * half_dims:]], axis=-1)

def gelu_pair(pre_act):
    normal_cdf = 0.5 * (1.0 + lax.erf(pre_act * (1.0 / math.sqrt(2.0))))
    density = jnp.exp(-0.5 * pre_act * pre_act) * (1.0 / math.sqrt(2.0 * math.pi))
    return (pre_act * normal_cdf, normal_cdf + pre_act * density)

def adam_update(weight, moments, gradient, clip_factor):
    clipped = gradient * clip_factor
    first_new = beta_one * moments[0] + (1.0 - beta_one) * clipped
    second_new = beta_two * moments[1] + (1.0 - beta_two) * clipped * clipped
    fix_first = 1.0 - math.pow(beta_one, STEP)
    fix_second = 1.0 - math.pow(beta_two, STEP)
    direction = first_new / fix_first / (jnp.sqrt(second_new / fix_second) + adam_eps)
    return (weight - learn_rate * (direction + decay_rate * weight), jnp.stack([first_new, second_new]))

def sequence_pass(seq_rows, seq_cot, segment_row, qkv_work, proj_work, up_work, down_work, vec_work):
    head_count = D // HD
    score_scale = 1.0 / math.sqrt(HD)
    length_all = seq_rows.shape[0]
    normed_one, unit_one, inverse_one = norm_rows(seq_rows, vec_work[0], vec_work[1])
    hidden_one = rounded(normed_one)
    mixed_rows = jnp.dot(hidden_one, qkv_work, preferred_element_type=jnp.float32)
    query_raw = (mixed_rows[:, :D] + vec_work[4]).reshape(length_all, head_count, HD)
    key_raw = mixed_rows[:, D:2 * D].reshape(length_all, head_count, HD)
    value_bf = rounded(mixed_rows[:, 2 * D:] + vec_work[5]).reshape(length_all, head_count, HD)
    cosine_table, sine_table = rotary_tables(doc_positions(segment_row), ROT)
    query_bf = rounded(rotate(query_raw, cosine_table, sine_table))
    key_bf = rounded(rotate(key_raw, cosine_table, sine_table))
    indices = jnp.arange(length_all, dtype=jnp.int32)
    allowed = (segment_row[:, None] == segment_row[None, :]) & (indices[None, :] <= indices[:, None])
    scores = jnp.einsum('qhd,khd->hqk', as_float(query_bf), as_float(key_bf)) * score_scale
    exp_scores = jnp.where(allowed[None], jnp.exp(scores), 0.0)
    totals = lax.optimization_barrier(jnp.sum(exp_scores, axis=-1))
    numerator = jnp.einsum('hqk,khd->qhd', as_float(rounded(exp_scores)), as_float(value_bf))
    attended = numerator / jnp.transpose(totals)[:, :, None]
    log_totals = jnp.log(totals)
    attended_bf = rounded(attended.reshape(length_all, D))
    proj_out = jnp.dot(attended_bf, proj_work, preferred_element_type=jnp.float32) + vec_work[6]
    normed_two, unit_two, inverse_two = norm_rows(seq_rows, vec_work[2], vec_work[3])
    hidden_two = rounded(normed_two)
    pre_act = jnp.dot(hidden_two, up_work, preferred_element_type=jnp.float32) + vec_work[8:].reshape(FF)
    act_values, act_slope = gelu_pair(pre_act)
    act_bf = rounded(act_values)
    mlp_out = jnp.dot(act_bf, down_work, preferred_element_type=jnp.float32) + vec_work[7]
    out_rows = seq_rows + proj_out + mlp_out
    cot_bf = rounded(seq_cot)
    down_part = jnp.dot(act_bf.T, cot_bf, preferred_element_type=jnp.float32)
    proj_part = jnp.dot(attended_bf.T, cot_bf, preferred_element_type=jnp.float32)
    cot_sum = lax.optimization_barrier(jnp.sum(seq_cot, axis=0))
    grad_pre = jnp.dot(cot_bf, down_work.T, preferred_element_type=jnp.float32) * act_slope
    grad_pre_bf = rounded(grad_pre)
    up_part = jnp.dot(hidden_two.T, grad_pre_bf, preferred_element_type=jnp.float32)
    rows_two, ln2_gain_part, ln2_bias_part = norm_back(jnp.dot(grad_pre_bf, up_work.T, preferred_element_type=jnp.float32), unit_two, inverse_two, vec_work[2])
    grad_att_bf = rounded(jnp.dot(cot_bf, proj_work.T, preferred_element_type=jnp.float32)).reshape(length_all, head_count, HD)
    probability = jnp.where(allowed[None], jnp.exp(scores - log_totals[:, :, None]), 0.0)
    grad_prob = jnp.einsum('qhd,khd->hqk', as_float(grad_att_bf), as_float(value_bf))
    row_delta = jnp.transpose(lax.optimization_barrier(jnp.sum(as_float(grad_att_bf) * attended, axis=-1)))
    grad_score = rounded(probability * (grad_prob - row_delta[:, :, None]) * score_scale)
    grad_query = jnp.einsum('hqk,khd->qhd', as_float(grad_score), as_float(key_bf))
    grad_key = jnp.einsum('hqk,qhd->khd', as_float(grad_score), as_float(query_bf))
    grad_value = jnp.einsum('hqk,qhd->khd', as_float(rounded(probability)), as_float(grad_att_bf))
    grad_query = rotate(grad_query, cosine_table, -sine_table).reshape(length_all, D)
    grad_key = rotate(grad_key, cosine_table, -sine_table).reshape(length_all, D)
    grad_value = grad_value.reshape(length_all, D)
    grad_mixed_bf = rounded(jnp.concatenate([grad_query, grad_key, grad_value], axis=1))
    qkv_part = jnp.dot(hidden_one.T, grad_mixed_bf, preferred_element_type=jnp.float32)
    rows_one, ln1_gain_part, ln1_bias_part = norm_back(jnp.dot(grad_mixed_bf, qkv_work.T, preferred_element_type=jnp.float32), unit_one, inverse_one, vec_work[0])
    in_grad = seq_cot + rows_one + rows_two
    vec_part = jnp.concatenate([jnp.stack([ln1_gain_part, ln1_bias_part, ln2_gain_part, ln2_bias_part, lax.optimization_barrier(jnp.sum(grad_query, axis=0)), lax.optimization_barrier(jnp.sum(grad_value, axis=0)), cot_sum, cot_sum]), lax.optimization_barrier(jnp.sum(grad_pre, axis=0)).reshape(FF // D, D)], axis=0)
    return (out_rows, in_grad, (qkv_part, proj_part, up_part, down_part, vec_part))

def reference(tokens, out_grad, segment_ids, qkv_weight, proj_weight, up_weight, down_weight, vectors, qkv_moments, proj_moments, up_moments, down_moments, vector_moments):
    qkv_work = qkv_weight.astype(jnp.bfloat16)
    proj_work = proj_weight.astype(jnp.bfloat16)
    up_work = up_weight.astype(jnp.bfloat16)
    down_work = down_weight.astype(jnp.bfloat16)
    vec_work = as_float(rounded(vectors))
    seq_tokens = tokens.reshape(SEQS, SEQ_LEN, D)
    seq_cots = out_grad.reshape(SEQS, SEQ_LEN, D)
    zero_grads = (jnp.zeros((D, 3 * D), jnp.float32), jnp.zeros((D, D), jnp.float32), jnp.zeros((D, FF), jnp.float32), jnp.zeros((FF, D), jnp.float32), jnp.zeros((VROWS, D), jnp.float32))

    def one_sequence(running, inputs):
        seq_rows, seq_cot, segment_row = inputs
        out_rows, in_grad, grads = sequence_pass(seq_rows, seq_cot, segment_row, qkv_work, proj_work, up_work, down_work, vec_work)
        return (jax.tree.map(lambda summed, latest: summed + latest, running, grads), (out_rows, in_grad))
    totals_grad, (out_seq, grad_seq) = lax.scan(one_sequence, zero_grads, (seq_tokens, seq_cots, segment_ids))
    qkv_grad, proj_grad, up_grad, down_grad, vectors_grad = totals_grad
    square_total = jnp.sum(qkv_grad * qkv_grad) + jnp.sum(proj_grad * proj_grad) + jnp.sum(up_grad * up_grad) + jnp.sum(down_grad * down_grad) + jnp.sum(vectors_grad * vectors_grad)
    norm_limit = math.sqrt(NPARAM)
    clip_factor = norm_limit / jnp.maximum(jnp.sqrt(square_total), norm_limit)
    qkv_new, qkv_moments_new = adam_update(qkv_weight, qkv_moments, qkv_grad, clip_factor)
    proj_new, proj_moments_new = adam_update(proj_weight, proj_moments, proj_grad, clip_factor)
    up_new, up_moments_new = adam_update(up_weight, up_moments, up_grad, clip_factor)
    down_new, down_moments_new = adam_update(down_weight, down_moments, down_grad, clip_factor)
    vectors_new, vector_moments_new = adam_update(vectors, vector_moments, vectors_grad, clip_factor)
    return (out_seq.reshape(TOKENS, D), grad_seq.reshape(TOKENS, D), qkv_grad, proj_grad, up_grad, down_grad, vectors_grad, qkv_new, proj_new, up_new, down_new, vectors_new, qkv_moments_new, proj_moments_new, up_moments_new, down_moments_new, vector_moments_new)
```

```python
import math

import jax
import jax.numpy as jnp
from jax import lax
from jax.sharding import PartitionSpec as P

D = 1024
FF = 4096
HD = 64
ROT = 16
STEP = 4
VROWS = 12
NPARAM = 12595200


ln_eps = 1e-05
beta_one = 0.9
beta_two = 0.95
learn_rate = 0.005
decay_rate = 0.01
adam_eps = 1e-08
rope_base = 10000.0


def norm_rows(inputs, gain_row, bias_row):
    center = inputs - jnp.mean(inputs, axis=-1, keepdims=True)
    inverse = lax.rsqrt(jnp.mean(center * center, axis=-1, keepdims=True) + ln_eps)
    unit_rows = center * inverse
    return (unit_rows * gain_row + bias_row, unit_rows, inverse)


def norm_back(upstream, unit_rows, inverse, gain_row):
    gain_grad = jnp.sum(upstream * unit_rows, axis=0)
    bias_grad = jnp.sum(upstream, axis=0)
    scaled_up = upstream * gain_row
    mean_plain = jnp.mean(scaled_up, axis=-1, keepdims=True)
    mean_unit = jnp.mean(scaled_up * unit_rows, axis=-1, keepdims=True)
    return (inverse * (scaled_up - mean_plain - unit_rows * mean_unit), gain_grad, bias_grad)


def doc_positions(segment_row):
    length_all = segment_row.shape[0]
    indices = jnp.arange(length_all, dtype=jnp.int32)
    starting = jnp.concatenate(
        [jnp.ones((1,), dtype=jnp.bool_), segment_row[1:] != segment_row[:-1]]
    )
    begins = lax.cummax(jnp.where(starting, indices, 0), axis=0)
    return indices - begins


def rotary_tables(positions, rot_dims):
    half_dims = rot_dims // 2
    exponent = jnp.arange(half_dims, dtype=jnp.float32) * (2.0 / rot_dims)
    inverse_freq = jnp.exp(-math.log(rope_base) * exponent)
    angles = positions.astype(jnp.float32)[:, None] * inverse_freq[None, :]
    return (jnp.cos(angles)[:, None, :], jnp.sin(angles)[:, None, :])


def rotate(head_rows, cosine_table, sine_table):
    half_dims = cosine_table.shape[-1]
    lower_half = head_rows[..., :half_dims]
    upper_half = head_rows[..., half_dims : 2 * half_dims]
    return jnp.concatenate(
        [
            lower_half * cosine_table - upper_half * sine_table,
            upper_half * cosine_table + lower_half * sine_table,
            head_rows[..., 2 * half_dims :],
        ],
        axis=-1,
    )


def gelu_pair(pre_act):
    normal_cdf = 0.5 * (1.0 + lax.erf(pre_act * (1.0 / math.sqrt(2.0))))
    density = jnp.exp(-0.5 * pre_act * pre_act) * (1.0 / math.sqrt(2.0 * math.pi))
    return (pre_act * normal_cdf, normal_cdf + pre_act * density)


def times_transposed(left, right):
    return lax.dot_general(
        left, right, (((1,), (1,)), ((), ())), preferred_element_type=jnp.float32
    )


def transposed_times(left, right):
    return lax.dot_general(
        left, right, (((0,), (0,)), ((), ())), preferred_element_type=jnp.float32
    )


def adam_update(weight, moments, gradient, clip_factor):
    clipped = gradient * clip_factor
    first_new = beta_one * moments[0] + (1.0 - beta_one) * clipped
    second_new = beta_two * moments[1] + (1.0 - beta_two) * clipped * clipped
    fix_first = 1.0 - math.pow(beta_one, STEP)
    fix_second = 1.0 - math.pow(beta_two, STEP)
    direction = first_new / fix_first / (jnp.sqrt(second_new / fix_second) + adam_eps)
    return (
        weight - learn_rate * (direction + decay_rate * weight),
        jnp.stack([first_new, second_new]),
    )


def plain_shards(
    tokens,
    out_grad,
    segment_ids,
    qkv_weight,
    proj_weight,
    up_weight,
    down_weight,
    vectors,
    qkv_moments,
    proj_moments,
    up_moments,
    down_moments,
    vector_moments,
):
    columns_full = (
        lax.all_gather(qkv_weight.astype(jnp.bfloat16), "shard", axis=1, tiled=True),
        lax.all_gather(proj_weight.astype(jnp.bfloat16), "shard", axis=1, tiled=True),
        lax.all_gather(up_weight.astype(jnp.bfloat16), "shard", axis=1, tiled=True),
        lax.all_gather(down_weight.astype(jnp.bfloat16), "shard", axis=1, tiled=True),
        lax.all_gather(vectors.astype(jnp.bfloat16), "shard", axis=1, tiled=True),
    )
    qkv_work, proj_work, up_work, down_work, vec_bf = (
        lax.all_gather(columns_full[0], "dp", axis=0, tiled=True),
        lax.all_gather(columns_full[1], "dp", axis=0, tiled=True),
        lax.all_gather(columns_full[2], "dp", axis=0, tiled=True),
        lax.all_gather(columns_full[3], "dp", axis=0, tiled=True),
        lax.all_gather(columns_full[4], "dp", axis=1, tiled=True),
    )
    vec_work = vec_bf.astype(jnp.float32)
    head_count = D // HD
    score_scale = 1.0 / math.sqrt(HD)
    local_rows = tokens.shape[0]
    segment_row = segment_ids[0]
    length_all = segment_row.shape[0]
    row_start = lax.axis_index("shard") * local_rows
    query_index = row_start + jnp.arange(local_rows, dtype=jnp.int32)
    query_segment = lax.dynamic_slice_in_dim(segment_row, row_start, local_rows)
    positions = lax.dynamic_slice_in_dim(doc_positions(segment_row), row_start, local_rows)
    normed_one, unit_one, inverse_one = norm_rows(tokens, vec_work[0], vec_work[1])
    hidden_one = normed_one.astype(jnp.bfloat16)
    mixed_rows = jnp.dot(hidden_one, qkv_work, preferred_element_type=jnp.float32)
    query_raw = (mixed_rows[:, :D] + vec_work[4]).reshape(local_rows, head_count, HD)
    key_raw = mixed_rows[:, D : 2 * D].reshape(local_rows, head_count, HD)
    value_bf = (mixed_rows[:, 2 * D :] + vec_work[5]).astype(jnp.bfloat16)
    cosine_table, sine_table = rotary_tables(positions, ROT)
    query_bf = rotate(query_raw, cosine_table, sine_table).astype(jnp.bfloat16)
    key_bf = rotate(key_raw, cosine_table, sine_table).astype(jnp.bfloat16).reshape(local_rows, D)
    key_piece = lax.all_gather(key_bf, "shard", axis=0, tiled=True)
    value_piece = lax.all_gather(value_bf, "shard", axis=0, tiled=True)
    piece_rows = key_piece.shape[0]
    key_heads = key_piece.reshape(piece_rows, head_count, HD)
    value_heads = value_piece.reshape(piece_rows, head_count, HD)
    key_index = jnp.arange(piece_rows, dtype=jnp.int32)
    allowed = (segment_row[None, :] == query_segment[:, None]) & (
        key_index[None, :] <= query_index[:, None]
    )
    scores = (
        jnp.einsum("qhd,khd->hqk", query_bf, key_heads, preferred_element_type=jnp.float32)
        * score_scale
    )
    exp_scores = jnp.where(allowed[None], jnp.exp(scores), 0.0)
    numerator = jnp.einsum(
        "hqk,khd->qhd",
        exp_scores.astype(jnp.bfloat16),
        value_heads,
        preferred_element_type=jnp.float32,
    )
    numerator, totals = (numerator, jnp.sum(exp_scores, axis=-1))
    attended = numerator / jnp.transpose(totals)[:, :, None]
    log_totals = jnp.log(totals)
    attended_bf = attended.reshape(local_rows, D).astype(jnp.bfloat16)
    proj_out = jnp.dot(attended_bf, proj_work, preferred_element_type=jnp.float32) + vec_work[6]
    normed_two, unit_two, inverse_two = norm_rows(tokens, vec_work[2], vec_work[3])
    hidden_two = normed_two.astype(jnp.bfloat16)
    pre_act = jnp.dot(hidden_two, up_work, preferred_element_type=jnp.float32) + vec_work[
        8:
    ].reshape(FF)
    act_values, act_slope = gelu_pair(pre_act)
    act_bf = act_values.astype(jnp.bfloat16)
    block_out = (
        tokens
        + proj_out
        + (jnp.dot(act_bf, down_work, preferred_element_type=jnp.float32) + vec_work[7])
    )
    cot_bf = out_grad.astype(jnp.bfloat16)
    down_part = transposed_times(act_bf, cot_bf)
    proj_part = transposed_times(attended_bf, cot_bf)
    cot_sum = jnp.sum(out_grad, axis=0)
    grad_pre = times_transposed(cot_bf, down_work) * act_slope
    grad_pre_bf = grad_pre.astype(jnp.bfloat16)
    up_part = transposed_times(hidden_two, grad_pre_bf)
    rows_two, ln2_gain_part, ln2_bias_part = norm_back(
        times_transposed(grad_pre_bf, up_work), unit_two, inverse_two, vec_work[2]
    )
    grad_att_bf = (
        times_transposed(cot_bf, proj_work).astype(jnp.bfloat16).reshape(local_rows, head_count, HD)
    )
    keys_all, values_all = (
        lax.all_gather(key_bf, "shard", axis=0, tiled=True),
        lax.all_gather(value_bf, "shard", axis=0, tiled=True),
    )
    key_heads = keys_all.reshape(length_all, head_count, HD)
    value_heads = values_all.reshape(length_all, head_count, HD)
    key_index = jnp.arange(length_all, dtype=jnp.int32)
    allowed = (segment_row[None, :] == query_segment[:, None]) & (
        key_index[None, :] <= query_index[:, None]
    )
    scores = (
        jnp.einsum("qhd,khd->hqk", query_bf, key_heads, preferred_element_type=jnp.float32)
        * score_scale
    )
    probability = jnp.where(allowed[None], jnp.exp(scores - log_totals[:, :, None]), 0.0)
    grad_prob = jnp.einsum(
        "qhd,khd->hqk", grad_att_bf, value_heads, preferred_element_type=jnp.float32
    )
    row_delta = jnp.transpose(jnp.sum(grad_att_bf.astype(jnp.float32) * attended, axis=-1))
    grad_score = (probability * (grad_prob - row_delta[:, :, None]) * score_scale).astype(
        jnp.bfloat16
    )
    grad_query = jnp.einsum(
        "hqk,khd->qhd", grad_score, key_heads, preferred_element_type=jnp.float32
    )
    grad_query = rotate(grad_query, cosine_table, -sine_table).reshape(local_rows, D)
    key_terms = jnp.einsum(
        "hqk,qhd->khd", grad_score, query_bf, preferred_element_type=jnp.float32
    ).reshape(length_all, D)
    value_terms = jnp.einsum(
        "hqk,qhd->khd",
        probability.astype(jnp.bfloat16),
        grad_att_bf,
        preferred_element_type=jnp.float32,
    ).reshape(length_all, D)
    key_value_grad = lax.psum_scatter(
        jnp.concatenate([key_terms, value_terms], axis=1), "shard", scatter_dimension=0, tiled=True
    )
    grad_key = rotate(
        key_value_grad[:, :D].reshape(local_rows, head_count, HD), cosine_table, -sine_table
    ).reshape(local_rows, D)
    grad_value = key_value_grad[:, D:]
    grad_mixed_bf = jnp.concatenate([grad_query, grad_key, grad_value], axis=1).astype(jnp.bfloat16)
    qkv_part = transposed_times(hidden_one, grad_mixed_bf)
    rows_one, ln1_gain_part, ln1_bias_part = norm_back(
        times_transposed(grad_mixed_bf, qkv_work), unit_one, inverse_one, vec_work[0]
    )
    tokens_grad = out_grad + rows_one + rows_two
    vec_part = jnp.concatenate(
        [
            jnp.stack(
                [
                    ln1_gain_part,
                    ln1_bias_part,
                    ln2_gain_part,
                    ln2_bias_part,
                    jnp.sum(grad_query, axis=0),
                    jnp.sum(grad_value, axis=0),
                    cot_sum,
                    cot_sum,
                ]
            ),
            jnp.sum(grad_pre, axis=0).reshape(FF // D, D),
        ],
        axis=0,
    )
    groups = lax.axis_size("dp")
    members = lax.axis_size("shard")
    owners = groups * members
    vec_split = vec_part.reshape(VROWS, groups, members, D // owners)
    group_sums = (
        lax.psum_scatter(qkv_part, "shard", scatter_dimension=1, tiled=True),
        lax.psum_scatter(proj_part, "shard", scatter_dimension=1, tiled=True),
        lax.psum_scatter(up_part, "shard", scatter_dimension=1, tiled=True),
        lax.psum_scatter(down_part, "shard", scatter_dimension=1, tiled=True),
        lax.psum_scatter(vec_split, "shard", scatter_dimension=2, tiled=True),
    )
    owner_sums = (
        lax.psum_scatter(group_sums[0], "dp", scatter_dimension=0, tiled=True),
        lax.psum_scatter(group_sums[1], "dp", scatter_dimension=0, tiled=True),
        lax.psum_scatter(group_sums[2], "dp", scatter_dimension=0, tiled=True),
        lax.psum_scatter(group_sums[3], "dp", scatter_dimension=0, tiled=True),
        lax.psum_scatter(group_sums[4], "dp", scatter_dimension=1, tiled=True),
    )
    qkv_grad = owner_sums[0]
    proj_grad = owner_sums[1]
    up_grad = owner_sums[2]
    down_grad = owner_sums[3]
    vectors_grad = owner_sums[4].reshape(VROWS, D // owners)
    local_square = (
        jnp.sum(qkv_grad * qkv_grad)
        + jnp.sum(proj_grad * proj_grad)
        + jnp.sum(up_grad * up_grad)
        + jnp.sum(down_grad * down_grad)
        + jnp.sum(vectors_grad * vectors_grad)
    )
    square_total = lax.psum(local_square, ("dp", "shard"))
    norm_limit = math.sqrt(NPARAM)
    clip_factor = norm_limit / jnp.maximum(jnp.sqrt(square_total), norm_limit)
    qkv_new, qkv_moments_new = adam_update(qkv_weight, qkv_moments, qkv_grad, clip_factor)
    proj_new, proj_moments_new = adam_update(proj_weight, proj_moments, proj_grad, clip_factor)
    up_new, up_moments_new = adam_update(up_weight, up_moments, up_grad, clip_factor)
    down_new, down_moments_new = adam_update(down_weight, down_moments, down_grad, clip_factor)
    vectors_new, vector_moments_new = adam_update(
        vectors, vector_moments, vectors_grad, clip_factor
    )
    return (
        block_out,
        tokens_grad,
        qkv_grad,
        proj_grad,
        up_grad,
        down_grad,
        vectors_grad,
        qkv_new,
        proj_new,
        up_new,
        down_new,
        vectors_new,
        qkv_moments_new,
        proj_moments_new,
        up_moments_new,
        down_moments_new,
        vector_moments_new,
    )


def swap_shard(piece):
    return lax.ppermute(piece, "shard", [(0, 1), (1, 0)])


def pick(array, index, axis):
    return lax.dynamic_index_in_dim(array, index, axis=axis, keepdims=False)


def ordered(member, mine, theirs, axis):
    return jnp.where(
        member == 0,
        jnp.concatenate([mine, theirs], axis=axis),
        jnp.concatenate([theirs, mine], axis=axis),
    )


def parity_columns(piece, width, member):
    rows = piece.shape[0]
    blocks = piece.reshape(rows, -1, 2, width)
    keep = pick(blocks, member, 2)
    received = swap_shard(pick(blocks, 1 - member, 2))
    return ordered(member, keep, received, 1).reshape(rows, -1)


def owner_columns(piece, width, member):
    rows = piece.shape[0]
    halves = piece.reshape(rows, 2, -1, width)
    keep = pick(halves, member, 1)
    received = swap_shard(pick(halves, 1 - member, 1))
    return jnp.where(
        member == 0,
        jnp.stack([keep, received], axis=2),
        jnp.stack([received, keep], axis=2),
    ).reshape(rows, -1)


def cross_swap(piece, groups, member, core):
    pairs = []
    for k in range(groups // 2):
        pairs += [(4 * k + 2, 4 * k + 1), (4 * k + 1, 4 * k + 2)]
    received = lax.ppermute(piece, ("dp", "shard"), pairs)
    return jnp.where(member == core, piece, received)


def scatter_groups(part, groups):
    index = lax.axis_index("dp")
    columns = part.shape[-1]
    current = part.reshape(groups, -1, columns)
    bit = 1
    while bit < groups:
        mine = (index // bit) % 2
        halves = current.reshape(-1, 2, current.shape[-2], columns)
        sent = pick(halves, 1 - mine, 1).astype(jnp.bfloat16)
        received = lax.ppermute(sent, "dp", [(i, i ^ bit) for i in range(groups)])
        current = pick(halves, mine, 1) + received.astype(jnp.float32)
        bit *= 2
    return current.reshape(-1, columns)


def sum_everywhere(values, groups):
    bit = 1
    values = values + swap_shard(values)
    while bit < groups:
        values = values + lax.ppermute(values, "dp", [(i, i ^ bit) for i in range(groups)])
        bit *= 2
    return values


def sum_halves(partial, member, local_rows):
    halves = partial.reshape(2, local_rows, partial.shape[-1])
    received = swap_shard(pick(halves, 1 - member, 0).astype(jnp.bfloat16))
    return pick(halves, member, 0) + received.astype(jnp.float32)


def spread(values, width, member):
    blocks = values.reshape(-1, 1, width)
    chosen = jnp.arange(2, dtype=jnp.int32)[None, :, None] == member
    return jnp.where(chosen, blocks, 0.0).reshape(-1)


def shards(
    tokens,
    out_grad,
    segment_ids,
    qkv_weight,
    proj_weight,
    up_weight,
    down_weight,
    vectors,
    qkv_moments,
    proj_moments,
    up_moments,
    down_moments,
    vector_moments,
):
    groups = lax.axis_size("dp")
    members = lax.axis_size("shard")
    head_count = D // HD
    if members != 2 or groups != head_count:
        return plain_shards(
            tokens,
            out_grad,
            segment_ids,
            qkv_weight,
            proj_weight,
            up_weight,
            down_weight,
            vectors,
            qkv_moments,
            proj_moments,
            up_moments,
            down_moments,
            vector_moments,
        )
    member = lax.axis_index("shard")
    group = lax.axis_index("dp")
    core = group % 2
    local_heads = head_count // 2
    half = D // 2
    local_rows = tokens.shape[0]
    unit_width = FF // groups // 2

    vec_work = lax.all_gather(
        vectors.astype(jnp.bfloat16), ("dp", "shard"), axis=1, tiled=True
    ).astype(jnp.float32)
    qkv_piece = parity_columns(qkv_weight.astype(jnp.bfloat16), HD, member)
    qkv_work = lax.all_gather(qkv_piece, "dp", axis=0, tiled=True)
    up_piece = parity_columns(up_weight.astype(jnp.bfloat16), unit_width, member)
    up_work = lax.all_gather(up_piece, "dp", axis=0, tiled=True)
    down_blocks = down_weight.astype(jnp.bfloat16).reshape(2, unit_width, half)
    down_piece = ordered(
        member,
        pick(down_blocks, member, 0),
        swap_shard(pick(down_blocks, 1 - member, 0)),
        1,
    )
    down_work = lax.all_gather(down_piece, "dp", axis=0, tiled=True)
    proj_piece = cross_swap(proj_weight.astype(jnp.bfloat16), groups, member, core)
    proj_work = (
        lax.all_gather(proj_piece, "dp", axis=0, tiled=True)
        .reshape(local_heads, 2, HD, half)
        .transpose(0, 2, 1, 3)
        .reshape(half, D)
    )

    segment_row = segment_ids[0]
    length_all = segment_row.shape[0]
    positions = doc_positions(segment_row)

    unit_rows_one = norm_rows(tokens, vec_work[0], vec_work[1])
    normed_one, unit_one, inverse_one = unit_rows_one
    normed_two, unit_two, inverse_two = norm_rows(tokens, vec_work[2], vec_work[3])

    def both(mine):
        return ordered(member, mine, swap_shard(mine), 0)

    cot_bf = both(out_grad.astype(jnp.bfloat16))
    hidden_one = both(normed_one.astype(jnp.bfloat16))
    hidden_two = both(normed_two.astype(jnp.bfloat16))

    q_bias = pick(vec_work[4].reshape(local_heads, 2, HD), member, 1).reshape(-1)
    v_bias = pick(vec_work[5].reshape(local_heads, 2, HD), member, 1).reshape(-1)
    up_bias = pick(vec_work[8:].reshape(groups, 2, unit_width), member, 1).reshape(-1)

    mixed_rows = jnp.dot(hidden_one, qkv_work, preferred_element_type=jnp.float32)
    score_scale = 1.0 / math.sqrt(HD)
    query_raw = (mixed_rows[:, :half] + q_bias).reshape(length_all, local_heads, HD)
    key_raw = mixed_rows[:, half : 2 * half].reshape(length_all, local_heads, HD)
    value_heads = (
        (mixed_rows[:, 2 * half :] + v_bias)
        .astype(jnp.bfloat16)
        .reshape(length_all, local_heads, HD)
    )
    cosine_table, sine_table = rotary_tables(positions, ROT)
    query_bf = rotate(query_raw, cosine_table, sine_table).astype(jnp.bfloat16)
    key_heads = rotate(key_raw, cosine_table, sine_table).astype(jnp.bfloat16)
    indices = jnp.arange(length_all, dtype=jnp.int32)
    allowed = (segment_row[None, :] == segment_row[:, None]) & (
        indices[None, :] <= indices[:, None]
    )
    scores = (
        jnp.einsum("qhd,khd->hqk", query_bf, key_heads, preferred_element_type=jnp.float32)
        * score_scale
    )
    exp_scores = jnp.where(allowed[None], jnp.exp(scores), 0.0)
    numerator = jnp.einsum(
        "hqk,khd->qhd",
        exp_scores.astype(jnp.bfloat16),
        value_heads,
        preferred_element_type=jnp.float32,
    )
    totals = jnp.sum(exp_scores, axis=-1)
    attended = numerator / jnp.transpose(totals)[:, :, None]
    log_totals = jnp.log(totals)
    attended_bf = attended.reshape(length_all, half).astype(jnp.bfloat16)
    grad_att_bf = times_transposed(cot_bf, proj_work).astype(jnp.bfloat16)
    proj_part = transposed_times(attended_bf, cot_bf)

    pre_act = jnp.dot(hidden_two, up_work, preferred_element_type=jnp.float32) + up_bias
    act_values, act_slope = gelu_pair(pre_act)
    act_bf = act_values.astype(jnp.bfloat16)
    grad_pre = times_transposed(cot_bf, down_work) * act_slope
    grad_pre_bf = grad_pre.astype(jnp.bfloat16)
    down_part = transposed_times(act_bf, cot_bf)
    up_part = transposed_times(hidden_two, grad_pre_bf)

    out_partial = jnp.dot(
        attended_bf, proj_work, preferred_element_type=jnp.float32
    ) + jnp.dot(act_bf, down_work, preferred_element_type=jnp.float32)
    block_out = (
        tokens + sum_halves(out_partial, member, local_rows) + vec_work[6] + vec_work[7]
    )
    rows_two, ln2_gain_part, ln2_bias_part = norm_back(
        sum_halves(times_transposed(grad_pre_bf, up_work), member, local_rows),
        unit_two,
        inverse_two,
        vec_work[2],
    )
    cot_sum = jnp.sum(out_grad, axis=0)
    grad_att_heads = grad_att_bf.reshape(length_all, local_heads, HD)
    probability = jnp.where(allowed[None], jnp.exp(scores - log_totals[:, :, None]), 0.0)
    grad_prob = jnp.einsum(
        "qhd,khd->hqk", grad_att_heads, value_heads, preferred_element_type=jnp.float32
    )
    row_delta = jnp.transpose(jnp.sum(grad_att_heads.astype(jnp.float32) * attended, axis=-1))
    grad_score = (probability * (grad_prob - row_delta[:, :, None]) * score_scale).astype(
        jnp.bfloat16
    )
    grad_query = jnp.einsum(
        "hqk,khd->qhd", grad_score, key_heads, preferred_element_type=jnp.float32
    )
    grad_query = rotate(grad_query, cosine_table, -sine_table).reshape(length_all, half)
    grad_key = jnp.einsum(
        "hqk,qhd->khd", grad_score, query_bf, preferred_element_type=jnp.float32
    )
    grad_key = rotate(grad_key, cosine_table, -sine_table).reshape(length_all, half)
    grad_value = jnp.einsum(
        "hqk,qhd->khd",
        probability.astype(jnp.bfloat16),
        grad_att_heads,
        preferred_element_type=jnp.float32,
    ).reshape(length_all, half)
    q_bias_part = jnp.sum(grad_query, axis=0)
    v_bias_part = jnp.sum(grad_value, axis=0)
    grad_mixed_bf = jnp.concatenate([grad_query, grad_key, grad_value], axis=1).astype(
        jnp.bfloat16
    )
    qkv_part = transposed_times(hidden_one, grad_mixed_bf)
    rows_one, ln1_gain_part, ln1_bias_part = norm_back(
        sum_halves(times_transposed(grad_mixed_bf, qkv_work), member, local_rows),
        unit_one,
        inverse_one,
        vec_work[0],
    )
    tokens_grad = out_grad + rows_one + rows_two
    vec_part = jnp.concatenate(
        [
            jnp.stack(
                [
                    ln1_gain_part,
                    ln1_bias_part,
                    ln2_gain_part,
                    ln2_bias_part,
                    spread(q_bias_part, HD, member),
                    spread(v_bias_part, HD, member),
                    cot_sum,
                    cot_sum,
                ]
            ),
            spread(jnp.sum(grad_pre, axis=0), unit_width, member).reshape(FF // D, D),
        ],
        axis=0,
    )
    vec_width = vectors.shape[1]
    vectors_grad = lax.dynamic_slice_in_dim(
        sum_everywhere(vec_part, groups), (group * 2 + member) * vec_width, vec_width, axis=1
    )

    down_rows = scatter_groups(down_part, groups).reshape(unit_width, 2, half)
    down_keep = pick(down_rows, member, 1)
    down_received = swap_shard(pick(down_rows, 1 - member, 1))
    down_grad = ordered(member, down_keep, down_received, 0)
    up_grad = owner_columns(scatter_groups(up_part, groups), unit_width, member)
    proj_chunks = proj_part.reshape(local_heads, HD, 2, half).transpose(0, 2, 1, 3)
    proj_grad = cross_swap(
        scatter_groups(proj_chunks.reshape(groups * HD, half), groups), groups, member, core
    )
    qkv_grad = owner_columns(scatter_groups(qkv_part, groups), HD, member)

    local_square = (
        jnp.sum(qkv_grad * qkv_grad)
        + jnp.sum(proj_grad * proj_grad)
        + jnp.sum(up_grad * up_grad)
        + jnp.sum(down_grad * down_grad)
        + jnp.sum(vectors_grad * vectors_grad)
    )
    square_total = sum_everywhere(jnp.broadcast_to(local_square, (8, 128)), groups)[0, 0]
    norm_limit = math.sqrt(NPARAM)
    clip_factor = norm_limit / jnp.maximum(jnp.sqrt(square_total), norm_limit)
    qkv_new, qkv_moments_new = adam_update(qkv_weight, qkv_moments, qkv_grad, clip_factor)
    proj_new, proj_moments_new = adam_update(proj_weight, proj_moments, proj_grad, clip_factor)
    up_new, up_moments_new = adam_update(up_weight, up_moments, up_grad, clip_factor)
    down_new, down_moments_new = adam_update(down_weight, down_moments, down_grad, clip_factor)
    vectors_new, vector_moments_new = adam_update(
        vectors, vector_moments, vectors_grad, clip_factor
    )
    return (
        block_out,
        tokens_grad,
        qkv_grad,
        proj_grad,
        up_grad,
        down_grad,
        vectors_grad,
        qkv_new,
        proj_new,
        up_new,
        down_new,
        vectors_new,
        qkv_moments_new,
        proj_moments_new,
        up_moments_new,
        down_moments_new,
        vector_moments_new,
    )


def solution(mesh):
    placed = (
        P(("dp", "shard"), None),
        P(("dp", "shard"), None),
        P("dp", None),
        P("dp", "shard"),
        P("dp", "shard"),
        P("dp", "shard"),
        P("dp", "shard"),
        P(None, ("dp", "shard")),
        P(None, "dp", "shard"),
        P(None, "dp", "shard"),
        P(None, "dp", "shard"),
        P(None, "dp", "shard"),
        P(None, None, ("dp", "shard")),
    )
    return jax.shard_map(
        shards,
        mesh=mesh,
        in_specs=placed,
        out_specs=(
            P(("dp", "shard"), None),
            P(("dp", "shard"), None),
            P("dp", "shard"),
            P("dp", "shard"),
            P("dp", "shard"),
            P("dp", "shard"),
            P(None, ("dp", "shard")),
            P("dp", "shard"),
            P("dp", "shard"),
            P("dp", "shard"),
            P("dp", "shard"),
            P(None, ("dp", "shard")),
            P(None, "dp", "shard"),
            P(None, "dp", "shard"),
            P(None, "dp", "shard"),
            P(None, "dp", "shard"),
            P(None, None, ("dp", "shard")),
        ),
        check_vma=False,
    )
```

```python
import math

import jax
import jax.numpy as jnp
from jax import lax
from jax.experimental import pallas as pl
from jax.experimental.pallas import tpu as pltpu
from jax.sharding import PartitionSpec as P

D = 1024
FF = 4096
HD = 64
ROT = 16
STEP = 4
VROWS = 12
NPARAM = 12595200


ln_eps = 1e-05
beta_one = 0.9
beta_two = 0.95
learn_rate = 0.005
decay_rate = 0.01
adam_eps = 1e-08
rope_base = 10000.0


def norm_rows(inputs, gain_row, bias_row):
    center = inputs - jnp.mean(inputs, axis=-1, keepdims=True)
    inverse = lax.rsqrt(jnp.mean(center * center, axis=-1, keepdims=True) + ln_eps)
    unit_rows = center * inverse
    return (unit_rows * gain_row + bias_row, unit_rows, inverse)


def norm_back(upstream, unit_rows, inverse, gain_row):
    gain_grad = jnp.sum(upstream * unit_rows, axis=0)
    bias_grad = jnp.sum(upstream, axis=0)
    scaled_up = upstream * gain_row
    mean_plain = jnp.mean(scaled_up, axis=-1, keepdims=True)
    mean_unit = jnp.mean(scaled_up * unit_rows, axis=-1, keepdims=True)
    return (inverse * (scaled_up - mean_plain - unit_rows * mean_unit), gain_grad, bias_grad)


def doc_positions(segment_row):
    length_all = segment_row.shape[0]
    indices = jnp.arange(length_all, dtype=jnp.int32)
    starting = jnp.concatenate(
        [jnp.ones((1,), dtype=jnp.bool_), segment_row[1:] != segment_row[:-1]]
    )
    begins = lax.cummax(jnp.where(starting, indices, 0), axis=0)
    return indices - begins


def rotary_tables(positions, rot_dims):
    half_dims = rot_dims // 2
    exponent = jnp.arange(half_dims, dtype=jnp.float32) * (2.0 / rot_dims)
    inverse_freq = jnp.exp(-math.log(rope_base) * exponent)
    angles = positions.astype(jnp.float32)[:, None] * inverse_freq[None, :]
    return (jnp.cos(angles)[:, None, :], jnp.sin(angles)[:, None, :])


def rotate(head_rows, cosine_table, sine_table):
    half_dims = cosine_table.shape[-1]
    lower_half = head_rows[..., :half_dims]
    upper_half = head_rows[..., half_dims : 2 * half_dims]
    return jnp.concatenate(
        [
            lower_half * cosine_table - upper_half * sine_table,
            upper_half * cosine_table + lower_half * sine_table,
            head_rows[..., 2 * half_dims :],
        ],
        axis=-1,
    )


def gelu_pair(pre_act):
    normal_cdf = 0.5 * (1.0 + lax.erf(pre_act * (1.0 / math.sqrt(2.0))))
    density = jnp.exp(-0.5 * pre_act * pre_act) * (1.0 / math.sqrt(2.0 * math.pi))
    return (pre_act * normal_cdf, normal_cdf + pre_act * density)


def times_transposed(left, right):
    return lax.dot_general(
        left, right, (((1,), (1,)), ((), ())), preferred_element_type=jnp.float32
    )


def transposed_times(left, right):
    return lax.dot_general(
        left, right, (((0,), (0,)), ((), ())), preferred_element_type=jnp.float32
    )


def adam_update(weight, moments, gradient, clip_factor):
    clipped = gradient * clip_factor
    first_new = beta_one * moments[0] + (1.0 - beta_one) * clipped
    second_new = beta_two * moments[1] + (1.0 - beta_two) * clipped * clipped
    fix_first = 1.0 - math.pow(beta_one, STEP)
    fix_second = 1.0 - math.pow(beta_two, STEP)
    direction = first_new / fix_first / (jnp.sqrt(second_new / fix_second) + adam_eps)
    return (
        weight - learn_rate * (direction + decay_rate * weight),
        jnp.stack([first_new, second_new]),
    )


def plain_shards(
    tokens,
    out_grad,
    segment_ids,
    qkv_weight,
    proj_weight,
    up_weight,
    down_weight,
    vectors,
    qkv_moments,
    proj_moments,
    up_moments,
    down_moments,
    vector_moments,
):
    columns_full = (
        lax.all_gather(qkv_weight.astype(jnp.bfloat16), "shard", axis=1, tiled=True),
        lax.all_gather(proj_weight.astype(jnp.bfloat16), "shard", axis=1, tiled=True),
        lax.all_gather(up_weight.astype(jnp.bfloat16), "shard", axis=1, tiled=True),
        lax.all_gather(down_weight.astype(jnp.bfloat16), "shard", axis=1, tiled=True),
        lax.all_gather(vectors.astype(jnp.bfloat16), "shard", axis=1, tiled=True),
    )
    qkv_work, proj_work, up_work, down_work, vec_bf = (
        lax.all_gather(columns_full[0], "dp", axis=0, tiled=True),
        lax.all_gather(columns_full[1], "dp", axis=0, tiled=True),
        lax.all_gather(columns_full[2], "dp", axis=0, tiled=True),
        lax.all_gather(columns_full[3], "dp", axis=0, tiled=True),
        lax.all_gather(columns_full[4], "dp", axis=1, tiled=True),
    )
    vec_work = vec_bf.astype(jnp.float32)
    head_count = D // HD
    score_scale = 1.0 / math.sqrt(HD)
    local_rows = tokens.shape[0]
    segment_row = segment_ids[0]
    length_all = segment_row.shape[0]
    row_start = lax.axis_index("shard") * local_rows
    query_index = row_start + jnp.arange(local_rows, dtype=jnp.int32)
    query_segment = lax.dynamic_slice_in_dim(segment_row, row_start, local_rows)
    positions = lax.dynamic_slice_in_dim(doc_positions(segment_row), row_start, local_rows)
    normed_one, unit_one, inverse_one = norm_rows(tokens, vec_work[0], vec_work[1])
    hidden_one = normed_one.astype(jnp.bfloat16)
    mixed_rows = jnp.dot(hidden_one, qkv_work, preferred_element_type=jnp.float32)
    query_raw = (mixed_rows[:, :D] + vec_work[4]).reshape(local_rows, head_count, HD)
    key_raw = mixed_rows[:, D : 2 * D].reshape(local_rows, head_count, HD)
    value_bf = (mixed_rows[:, 2 * D :] + vec_work[5]).astype(jnp.bfloat16)
    cosine_table, sine_table = rotary_tables(positions, ROT)
    query_bf = rotate(query_raw, cosine_table, sine_table).astype(jnp.bfloat16)
    key_bf = rotate(key_raw, cosine_table, sine_table).astype(jnp.bfloat16).reshape(local_rows, D)
    key_piece = lax.all_gather(key_bf, "shard", axis=0, tiled=True)
    value_piece = lax.all_gather(value_bf, "shard", axis=0, tiled=True)
    piece_rows = key_piece.shape[0]
    key_heads = key_piece.reshape(piece_rows, head_count, HD)
    value_heads = value_piece.reshape(piece_rows, head_count, HD)
    key_index = jnp.arange(piece_rows, dtype=jnp.int32)
    allowed = (segment_row[None, :] == query_segment[:, None]) & (
        key_index[None, :] <= query_index[:, None]
    )
    scores = (
        jnp.einsum("qhd,khd->hqk", query_bf, key_heads, preferred_element_type=jnp.float32)
        * score_scale
    )
    exp_scores = jnp.where(allowed[None], jnp.exp(scores), 0.0)
    numerator = jnp.einsum(
        "hqk,khd->qhd",
        exp_scores.astype(jnp.bfloat16),
        value_heads,
        preferred_element_type=jnp.float32,
    )
    numerator, totals = (numerator, jnp.sum(exp_scores, axis=-1))
    attended = numerator / jnp.transpose(totals)[:, :, None]
    log_totals = jnp.log(totals)
    attended_bf = attended.reshape(local_rows, D).astype(jnp.bfloat16)
    proj_out = jnp.dot(attended_bf, proj_work, preferred_element_type=jnp.float32) + vec_work[6]
    normed_two, unit_two, inverse_two = norm_rows(tokens, vec_work[2], vec_work[3])
    hidden_two = normed_two.astype(jnp.bfloat16)
    pre_act = jnp.dot(hidden_two, up_work, preferred_element_type=jnp.float32) + vec_work[
        8:
    ].reshape(FF)
    act_values, act_slope = gelu_pair(pre_act)
    act_bf = act_values.astype(jnp.bfloat16)
    block_out = (
        tokens
        + proj_out
        + (jnp.dot(act_bf, down_work, preferred_element_type=jnp.float32) + vec_work[7])
    )
    cot_bf = out_grad.astype(jnp.bfloat16)
    down_part = transposed_times(act_bf, cot_bf)
    proj_part = transposed_times(attended_bf, cot_bf)
    cot_sum = jnp.sum(out_grad, axis=0)
    grad_pre = times_transposed(cot_bf, down_work) * act_slope
    grad_pre_bf = grad_pre.astype(jnp.bfloat16)
    up_part = transposed_times(hidden_two, grad_pre_bf)
    rows_two, ln2_gain_part, ln2_bias_part = norm_back(
        times_transposed(grad_pre_bf, up_work), unit_two, inverse_two, vec_work[2]
    )
    grad_att_bf = (
        times_transposed(cot_bf, proj_work).astype(jnp.bfloat16).reshape(local_rows, head_count, HD)
    )
    keys_all, values_all = (
        lax.all_gather(key_bf, "shard", axis=0, tiled=True),
        lax.all_gather(value_bf, "shard", axis=0, tiled=True),
    )
    key_heads = keys_all.reshape(length_all, head_count, HD)
    value_heads = values_all.reshape(length_all, head_count, HD)
    key_index = jnp.arange(length_all, dtype=jnp.int32)
    allowed = (segment_row[None, :] == query_segment[:, None]) & (
        key_index[None, :] <= query_index[:, None]
    )
    scores = (
        jnp.einsum("qhd,khd->hqk", query_bf, key_heads, preferred_element_type=jnp.float32)
        * score_scale
    )
    probability = jnp.where(allowed[None], jnp.exp(scores - log_totals[:, :, None]), 0.0)
    grad_prob = jnp.einsum(
        "qhd,khd->hqk", grad_att_bf, value_heads, preferred_element_type=jnp.float32
    )
    row_delta = jnp.transpose(jnp.sum(grad_att_bf.astype(jnp.float32) * attended, axis=-1))
    grad_score = (probability * (grad_prob - row_delta[:, :, None]) * score_scale).astype(
        jnp.bfloat16
    )
    grad_query = jnp.einsum(
        "hqk,khd->qhd", grad_score, key_heads, preferred_element_type=jnp.float32
    )
    grad_query = rotate(grad_query, cosine_table, -sine_table).reshape(local_rows, D)
    key_terms = jnp.einsum(
        "hqk,qhd->khd", grad_score, query_bf, preferred_element_type=jnp.float32
    ).reshape(length_all, D)
    value_terms = jnp.einsum(
        "hqk,qhd->khd",
        probability.astype(jnp.bfloat16),
        grad_att_bf,
        preferred_element_type=jnp.float32,
    ).reshape(length_all, D)
    key_value_grad = lax.psum_scatter(
        jnp.concatenate([key_terms, value_terms], axis=1), "shard", scatter_dimension=0, tiled=True
    )
    grad_key = rotate(
        key_value_grad[:, :D].reshape(local_rows, head_count, HD), cosine_table, -sine_table
    ).reshape(local_rows, D)
    grad_value = key_value_grad[:, D:]
    grad_mixed_bf = jnp.concatenate([grad_query, grad_key, grad_value], axis=1).astype(jnp.bfloat16)
    qkv_part = transposed_times(hidden_one, grad_mixed_bf)
    rows_one, ln1_gain_part, ln1_bias_part = norm_back(
        times_transposed(grad_mixed_bf, qkv_work), unit_one, inverse_one, vec_work[0]
    )
    tokens_grad = out_grad + rows_one + rows_two
    vec_part = jnp.concatenate(
        [
            jnp.stack(
                [
                    ln1_gain_part,
                    ln1_bias_part,
                    ln2_gain_part,
                    ln2_bias_part,
                    jnp.sum(grad_query, axis=0),
                    jnp.sum(grad_value, axis=0),
                    cot_sum,
                    cot_sum,
                ]
            ),
            jnp.sum(grad_pre, axis=0).reshape(FF // D, D),
        ],
        axis=0,
    )
    groups = lax.axis_size("dp")
    members = lax.axis_size("shard")
    owners = groups * members
    vec_split = vec_part.reshape(VROWS, groups, members, D // owners)
    group_sums = (
        lax.psum_scatter(qkv_part, "shard", scatter_dimension=1, tiled=True),
        lax.psum_scatter(proj_part, "shard", scatter_dimension=1, tiled=True),
        lax.psum_scatter(up_part, "shard", scatter_dimension=1, tiled=True),
        lax.psum_scatter(down_part, "shard", scatter_dimension=1, tiled=True),
        lax.psum_scatter(vec_split, "shard", scatter_dimension=2, tiled=True),
    )
    owner_sums = (
        lax.psum_scatter(group_sums[0], "dp", scatter_dimension=0, tiled=True),
        lax.psum_scatter(group_sums[1], "dp", scatter_dimension=0, tiled=True),
        lax.psum_scatter(group_sums[2], "dp", scatter_dimension=0, tiled=True),
        lax.psum_scatter(group_sums[3], "dp", scatter_dimension=0, tiled=True),
        lax.psum_scatter(group_sums[4], "dp", scatter_dimension=1, tiled=True),
    )
    qkv_grad = owner_sums[0]
    proj_grad = owner_sums[1]
    up_grad = owner_sums[2]
    down_grad = owner_sums[3]
    vectors_grad = owner_sums[4].reshape(VROWS, D // owners)
    local_square = (
        jnp.sum(qkv_grad * qkv_grad)
        + jnp.sum(proj_grad * proj_grad)
        + jnp.sum(up_grad * up_grad)
        + jnp.sum(down_grad * down_grad)
        + jnp.sum(vectors_grad * vectors_grad)
    )
    square_total = lax.psum(local_square, ("dp", "shard"))
    norm_limit = math.sqrt(NPARAM)
    clip_factor = norm_limit / jnp.maximum(jnp.sqrt(square_total), norm_limit)
    qkv_new, qkv_moments_new = adam_update(qkv_weight, qkv_moments, qkv_grad, clip_factor)
    proj_new, proj_moments_new = adam_update(proj_weight, proj_moments, proj_grad, clip_factor)
    up_new, up_moments_new = adam_update(up_weight, up_moments, up_grad, clip_factor)
    down_new, down_moments_new = adam_update(down_weight, down_moments, down_grad, clip_factor)
    vectors_new, vector_moments_new = adam_update(
        vectors, vector_moments, vectors_grad, clip_factor
    )
    return (
        block_out,
        tokens_grad,
        qkv_grad,
        proj_grad,
        up_grad,
        down_grad,
        vectors_grad,
        qkv_new,
        proj_new,
        up_new,
        down_new,
        vectors_new,
        qkv_moments_new,
        proj_moments_new,
        up_moments_new,
        down_moments_new,
        vector_moments_new,
    )


def swap_shard(piece):
    return lax.ppermute(piece, "shard", [(0, 1), (1, 0)])


def pick(array, index, axis):
    return lax.dynamic_index_in_dim(array, index, axis=axis, keepdims=False)


def ordered(member, mine, theirs, axis):
    return jnp.where(
        member == 0,
        jnp.concatenate([mine, theirs], axis=axis),
        jnp.concatenate([theirs, mine], axis=axis),
    )


def parity_columns(piece, width, member):
    rows = piece.shape[0]
    blocks = piece.reshape(rows, -1, 2, width)
    keep = pick(blocks, member, 2)
    received = swap_shard(pick(blocks, 1 - member, 2))
    return ordered(member, keep, received, 1).reshape(rows, -1)


def owner_columns(piece, width, member):
    rows = piece.shape[0]
    halves = piece.reshape(rows, 2, -1, width)
    keep = pick(halves, member, 1)
    received = swap_shard(pick(halves, 1 - member, 1))
    return jnp.where(
        member == 0,
        jnp.stack([keep, received], axis=2),
        jnp.stack([received, keep], axis=2),
    ).reshape(rows, -1)


def cross_swap(piece, groups, member, core):
    pairs = []
    for k in range(groups // 2):
        pairs += [(4 * k + 2, 4 * k + 1), (4 * k + 1, 4 * k + 2)]
    received = lax.ppermute(piece, ("dp", "shard"), pairs)
    return jnp.where(member == core, piece, received)


def scatter_groups(part, groups):
    index = lax.axis_index("dp")
    columns = part.shape[-1]
    current = part.reshape(groups, -1, columns)
    bit = 1
    while bit < groups:
        mine = (index // bit) % 2
        halves = current.reshape(-1, 2, current.shape[-2], columns)
        sent = pick(halves, 1 - mine, 1).astype(jnp.bfloat16)
        received = lax.ppermute(sent, "dp", [(i, i ^ bit) for i in range(groups)])
        current = pick(halves, mine, 1) + received.astype(jnp.float32)
        bit *= 2
    return current.reshape(-1, columns)


def sum_everywhere(values, groups):
    bit = 1
    values = values + swap_shard(values)
    while bit < groups:
        values = values + lax.ppermute(values, "dp", [(i, i ^ bit) for i in range(groups)])
        bit *= 2
    return values


def sum_halves(partial, member, local_rows):
    halves = partial.reshape(2, local_rows, partial.shape[-1])
    received = swap_shard(pick(halves, 1 - member, 0).astype(jnp.bfloat16))
    return pick(halves, member, 0) + received.astype(jnp.float32)


def spread(values, width, member):
    blocks = values.reshape(-1, 1, width)
    chosen = jnp.arange(2, dtype=jnp.int32)[None, :, None] == member
    return jnp.where(chosen, blocks, 0.0).reshape(-1)


def rolled(rows, cosine, down_sine, up_sine):
    width = rows.shape[1]
    lower = pltpu.roll(rows, width - ROT // 2, 1)
    upper = pltpu.roll(rows, ROT // 2, 1)
    return rows * cosine + lower * down_sine + upper * up_sine


def split_pair(rows):
    lanes = lax.broadcasted_iota(jnp.int32, rows.shape, 1)
    return (
        jnp.where(lanes < HD, rows, jnp.zeros_like(rows)),
        jnp.where(lanes < HD, jnp.zeros_like(rows), rows),
    )


def block_mask(seg_column, seg_row, start, size, extent):
    rows = start + lax.broadcasted_iota(jnp.int32, (size, extent), 0)
    keys = lax.broadcasted_iota(jnp.int32, (size, extent), 1)
    same = seg_column[start : start + size, :] == seg_row[:, :extent]
    return same & (keys <= rows)


def attend_kernel(
    query_ref, key_ref, value_ref, q_bias_ref, v_bias_ref, cos_ref, down_ref, up_ref,
    column_ref, row_ref, query_out, key_out, value_out, att_out, att_bf_out, log_out,
):
    scale = 1.0 / math.sqrt(HD)
    length = query_ref.shape[0]
    size = length // 4
    cosine, down_sine, up_sine = cos_ref[...], down_ref[...], up_ref[...]
    query_out[...] = rolled(
        query_ref[...] + q_bias_ref[...], cosine, down_sine, up_sine
    ).astype(jnp.bfloat16)
    key_out[...] = rolled(key_ref[...], cosine, down_sine, up_sine).astype(jnp.bfloat16)
    value_out[...] = (value_ref[...] + v_bias_ref[...]).astype(jnp.bfloat16)
    for start in range(0, length, size):
        extent = start + size
        mask = block_mask(column_ref, row_ref, start, size, extent)
        keys, values = key_out[:extent, :], value_out[:extent, :]
        results = []
        for query in split_pair(query_out[start:extent, :].astype(jnp.float32)):
            scores = times_transposed(query.astype(jnp.bfloat16), keys) * scale
            exp_scores = jnp.where(mask, jnp.exp(scores), 0.0)
            totals = jnp.sum(exp_scores, axis=1, keepdims=True)
            numerator = jnp.dot(
                exp_scores.astype(jnp.bfloat16), values, preferred_element_type=jnp.float32
            )
            results.append((numerator / totals, jnp.log(totals)))
        lanes = lax.broadcasted_iota(jnp.int32, (size, 2 * HD), 1) < HD
        attended = jnp.where(lanes, results[0][0], results[1][0])
        att_out[start:extent, :] = attended
        att_bf_out[start:extent, :] = attended.astype(jnp.bfloat16)
        log_out[start:extent, :] = jnp.where(lanes, results[0][1], results[1][1])


def attend_back_kernel(
    query_ref, key_ref, value_ref, grad_ref, att_ref, log_ref, cos_ref, down_ref, up_ref,
    column_ref, row_ref, query_out, key_out, value_out, q_bias_out, v_bias_out,
    query_sum, key_sum, value_sum,
):
    scale = 1.0 / math.sqrt(HD)
    length = query_ref.shape[0]
    size = length // 4
    key_sum[...] = jnp.zeros_like(key_sum)
    value_sum[...] = jnp.zeros_like(value_sum)
    for start in range(0, length, size):
        extent = start + size
        mask = block_mask(column_ref, row_ref, start, size, extent)
        keys, values = key_ref[:extent, :], value_ref[:extent, :]
        queries = split_pair(query_ref[start:extent, :].astype(jnp.float32))
        grads = split_pair(grad_ref[start:extent, :].astype(jnp.float32))
        attended = att_ref[start:extent, :]
        pieces = []
        for head in range(2):
            query = queries[head].astype(jnp.bfloat16)
            grad = grads[head].astype(jnp.bfloat16)
            log_total = log_ref[start:extent, head * HD : head * HD + 1]
            scores = times_transposed(query, keys) * scale
            probability = jnp.where(mask, jnp.exp(scores - log_total), 0.0)
            grad_prob = times_transposed(grad, values)
            delta = jnp.sum(grads[head] * attended, axis=1, keepdims=True)
            grad_score = (probability * (grad_prob - delta) * scale).astype(jnp.bfloat16)
            pieces.append(jnp.dot(grad_score, keys, preferred_element_type=jnp.float32))
            key_sum[:extent, :] += transposed_times(grad_score, query)
            value_sum[:extent, :] += transposed_times(probability.astype(jnp.bfloat16), grad)
        lanes = lax.broadcasted_iota(jnp.int32, (size, 2 * HD), 1) < HD
        query_sum[start:extent, :] = jnp.where(lanes, pieces[0], pieces[1])
    cosine, down_sine, up_sine = cos_ref[...], down_ref[...], up_ref[...]
    grad_query = rolled(query_sum[...], cosine, -down_sine, -up_sine)
    query_out[...] = grad_query.astype(jnp.bfloat16)
    q_bias_out[...] = jnp.sum(grad_query, axis=0, keepdims=True)
    key_out[...] = rolled(key_sum[...], cosine, -down_sine, -up_sine).astype(jnp.bfloat16)
    grad_value = value_sum[...]
    value_out[...] = grad_value.astype(jnp.bfloat16)
    v_bias_out[...] = jnp.sum(grad_value, axis=0, keepdims=True)


def lane_tables(positions):
    dims = jnp.arange(2 * HD, dtype=jnp.int32) % HD
    half_dims = ROT // 2
    exponent = (dims % half_dims).astype(jnp.float32) * (2.0 / ROT)
    inverse_freq = jnp.exp(-math.log(rope_base) * exponent)
    angles = positions.astype(jnp.float32)[:, None] * inverse_freq[None, :]
    sine = jnp.sin(angles)
    return (
        jnp.where(dims[None] < ROT, jnp.cos(angles), 1.0),
        jnp.where(dims[None] < half_dims, -sine, 0.0),
        jnp.where((dims[None] >= half_dims) & (dims[None] < ROT), sine, 0.0),
    )


def pair_specs(length):
    def columns(offset):
        return pl.BlockSpec((length, 2 * HD), lambda j: (0, offset + j))

    table = pl.BlockSpec((length, 2 * HD), lambda j: (0, 0))
    bias = pl.BlockSpec((1, 2 * HD), lambda j: (0, j))
    seg_column = pl.BlockSpec((length, 1), lambda j: (0, 0))
    seg_row = pl.BlockSpec((1, length), lambda j: (0, 0))
    return columns, table, bias, seg_column, seg_row


def attend(mixed_rows, q_bias, v_bias, tables, segment_row):
    length = mixed_rows.shape[0]
    width = mixed_rows.shape[1] // 3
    pairs = width // (2 * HD)
    columns, table, bias, seg_column, seg_row = pair_specs(length)
    shapes = [jnp.bfloat16, jnp.bfloat16, jnp.bfloat16, jnp.float32, jnp.bfloat16, jnp.float32]
    flops = 4 * length * length * width
    return pl.pallas_call(
        attend_kernel,
        grid=(pairs,),
        in_specs=[columns(0), columns(pairs), columns(2 * pairs), bias, bias, table, table, table,
                  seg_column, seg_row],
        out_specs=[columns(0)] * 6,
        out_shape=[jax.ShapeDtypeStruct((length, width), kind) for kind in shapes],
        cost_estimate=pl.CostEstimate(
            flops=flops, bytes_accessed=24 * length * width, transcendentals=flops // (4 * HD)
        ),
        name="attend",
    )(mixed_rows, mixed_rows, mixed_rows, q_bias[None], v_bias[None], *tables,
      segment_row[:, None], segment_row[None, :])


def attend_back(query, key, value, grad, attended, log_totals, tables, segment_row):
    length, width = query.shape
    pairs = width // (2 * HD)
    columns, table, bias, seg_column, seg_row = pair_specs(length)
    flops = 10 * length * length * width
    return pl.pallas_call(
        attend_back_kernel,
        grid=(pairs,),
        in_specs=[columns(0)] * 6 + [table, table, table, seg_column, seg_row],
        out_specs=[columns(0)] * 3 + [bias, bias],
        out_shape=[jax.ShapeDtypeStruct((length, width), jnp.bfloat16)] * 3
        + [jax.ShapeDtypeStruct((1, width), jnp.float32)] * 2,
        scratch_shapes=[pltpu.VMEM((length, 2 * HD), jnp.float32)] * 3,
        cost_estimate=pl.CostEstimate(
            flops=flops, bytes_accessed=24 * length * width, transcendentals=flops // (10 * HD)
        ),
        name="attend_back",
    )(query, key, value, grad, attended, log_totals, *tables,
      segment_row[:, None], segment_row[None, :])


def gather_groups(piece, groups):
    index = lax.axis_index("dp")
    current = piece[None]
    bit = groups // 2
    while bit >= 1:
        low = (index // bit) % 2 == 0
        received = lax.ppermute(current, "dp", [(i, i ^ bit) for i in range(groups)])
        current = jnp.where(
            low,
            jnp.stack([current, received], axis=1),
            jnp.stack([received, current], axis=1),
        ).reshape((-1,) + piece.shape)
        bit //= 2
    return current


def shards(
    tokens,
    out_grad,
    segment_ids,
    qkv_weight,
    proj_weight,
    up_weight,
    down_weight,
    vectors,
    qkv_moments,
    proj_moments,
    up_moments,
    down_moments,
    vector_moments,
):
    groups = lax.axis_size("dp")
    members = lax.axis_size("shard")
    head_count = D // HD
    if members != 2 or groups != head_count:
        return plain_shards(
            tokens,
            out_grad,
            segment_ids,
            qkv_weight,
            proj_weight,
            up_weight,
            down_weight,
            vectors,
            qkv_moments,
            proj_moments,
            up_moments,
            down_moments,
            vector_moments,
        )
    member = lax.axis_index("shard")
    group = lax.axis_index("dp")
    core = group % 2
    local_heads = head_count // 2
    half = D // 2
    local_rows = tokens.shape[0]
    unit_width = FF // groups // 2

    vec_pair = vectors.astype(jnp.bfloat16)
    vec_pair = ordered(member, vec_pair, swap_shard(vec_pair), 1)
    vec_work = (
        gather_groups(vec_pair, groups).transpose(1, 0, 2).reshape(VROWS, D).astype(jnp.float32)
    )
    qkv_piece = parity_columns(qkv_weight.astype(jnp.bfloat16), HD, member)
    qkv_work = gather_groups(qkv_piece, groups).reshape(D, -1)
    up_piece = parity_columns(up_weight.astype(jnp.bfloat16), unit_width, member)
    up_work = lax.all_gather(up_piece, "dp", axis=0, tiled=True)
    down_blocks = down_weight.astype(jnp.bfloat16).reshape(2, unit_width, half)
    down_piece = ordered(
        member,
        pick(down_blocks, member, 0),
        swap_shard(pick(down_blocks, 1 - member, 0)),
        1,
    )
    down_work = lax.all_gather(down_piece, "dp", axis=0, tiled=True)
    proj_piece = cross_swap(proj_weight.astype(jnp.bfloat16), groups, member, core)
    proj_work = (
        gather_groups(proj_piece, groups)
        .reshape(local_heads, 2, HD, half)
        .transpose(0, 2, 1, 3)
        .reshape(half, D)
    )

    segment_row = segment_ids[0]
    length_all = segment_row.shape[0]
    positions = doc_positions(segment_row)

    unit_rows_one = norm_rows(tokens, vec_work[0], vec_work[1])
    normed_one, unit_one, inverse_one = unit_rows_one
    normed_two, unit_two, inverse_two = norm_rows(tokens, vec_work[2], vec_work[3])

    def both(mine):
        return ordered(member, mine, swap_shard(mine), 0)

    cot_bf = both(out_grad.astype(jnp.bfloat16))
    hidden_one = both(normed_one.astype(jnp.bfloat16))
    hidden_two = both(normed_two.astype(jnp.bfloat16))

    q_bias = pick(vec_work[4].reshape(local_heads, 2, HD), member, 1).reshape(-1)
    v_bias = pick(vec_work[5].reshape(local_heads, 2, HD), member, 1).reshape(-1)
    up_bias = pick(vec_work[8:].reshape(groups, 2, unit_width), member, 1).reshape(-1)

    mixed_rows = jnp.dot(hidden_one, qkv_work, preferred_element_type=jnp.float32)
    tables = lane_tables(positions)
    query_bf, key_bf, value_bf, attended, attended_bf, log_totals = attend(
        mixed_rows, q_bias, v_bias, tables, segment_row
    )
    grad_att_bf = times_transposed(cot_bf, proj_work).astype(jnp.bfloat16)
    proj_part = transposed_times(attended_bf, cot_bf)

    pre_act = jnp.dot(hidden_two, up_work, preferred_element_type=jnp.float32) + up_bias
    act_values, act_slope = gelu_pair(pre_act)
    act_bf = act_values.astype(jnp.bfloat16)
    grad_pre = times_transposed(cot_bf, down_work) * act_slope
    grad_pre_bf = grad_pre.astype(jnp.bfloat16)
    down_part = transposed_times(act_bf, cot_bf)
    up_part = transposed_times(hidden_two, grad_pre_bf)

    out_partial = jnp.dot(
        attended_bf, proj_work, preferred_element_type=jnp.float32
    ) + jnp.dot(act_bf, down_work, preferred_element_type=jnp.float32)
    block_out = (
        tokens + sum_halves(out_partial, member, local_rows) + vec_work[6] + vec_work[7]
    )
    rows_two, ln2_gain_part, ln2_bias_part = norm_back(
        sum_halves(times_transposed(grad_pre_bf, up_work), member, local_rows),
        unit_two,
        inverse_two,
        vec_work[2],
    )
    cot_sum = jnp.sum(out_grad, axis=0)
    grad_att_late, down_part, up_part = lax.optimization_barrier(
        (grad_att_bf, down_part, up_part)
    )
    grad_query, grad_key, grad_value, q_bias_part, v_bias_part = attend_back(
        query_bf, key_bf, value_bf, grad_att_late, attended, log_totals, tables, segment_row
    )
    q_bias_part, v_bias_part = q_bias_part[0], v_bias_part[0]
    grad_mixed_bf = jnp.concatenate([grad_query, grad_key, grad_value], axis=1)
    qkv_part = transposed_times(hidden_one, grad_mixed_bf)
    rows_one, ln1_gain_part, ln1_bias_part = norm_back(
        sum_halves(times_transposed(grad_mixed_bf, qkv_work), member, local_rows),
        unit_one,
        inverse_one,
        vec_work[0],
    )
    tokens_grad = out_grad + rows_one + rows_two
    vec_part = jnp.concatenate(
        [
            jnp.stack(
                [
                    ln1_gain_part,
                    ln1_bias_part,
                    ln2_gain_part,
                    ln2_bias_part,
                    spread(q_bias_part, HD, member),
                    spread(v_bias_part, HD, member),
                    cot_sum,
                    cot_sum,
                ]
            ),
            spread(jnp.sum(grad_pre, axis=0), unit_width, member).reshape(FF // D, D),
        ],
        axis=0,
    )
    vec_width = vectors.shape[1]
    vectors_grad = lax.dynamic_slice_in_dim(
        sum_everywhere(vec_part, groups), (group * 2 + member) * vec_width, vec_width, axis=1
    )

    down_rows = scatter_groups(down_part, groups).reshape(unit_width, 2, half)
    down_keep = pick(down_rows, member, 1)
    down_received = swap_shard(pick(down_rows, 1 - member, 1))
    down_grad = ordered(member, down_keep, down_received, 0)
    up_grad = owner_columns(scatter_groups(up_part, groups), unit_width, member)
    proj_chunks = proj_part.reshape(local_heads, HD, 2, half).transpose(0, 2, 1, 3)
    proj_grad = cross_swap(
        scatter_groups(proj_chunks.reshape(groups * HD, half), groups), groups, member, core
    )
    qkv_grad = owner_columns(scatter_groups(qkv_part, groups), HD, member)

    local_square = (
        jnp.sum(qkv_grad * qkv_grad)
        + jnp.sum(proj_grad * proj_grad)
        + jnp.sum(up_grad * up_grad)
        + jnp.sum(down_grad * down_grad)
        + jnp.sum(vectors_grad * vectors_grad)
    )
    square_total = sum_everywhere(jnp.broadcast_to(local_square, (8, 128)), groups)[0, 0]
    norm_limit = math.sqrt(NPARAM)
    clip_factor = norm_limit / jnp.maximum(jnp.sqrt(square_total), norm_limit)
    qkv_new, qkv_moments_new = adam_update(qkv_weight, qkv_moments, qkv_grad, clip_factor)
    proj_new, proj_moments_new = adam_update(proj_weight, proj_moments, proj_grad, clip_factor)
    up_new, up_moments_new = adam_update(up_weight, up_moments, up_grad, clip_factor)
    down_new, down_moments_new = adam_update(down_weight, down_moments, down_grad, clip_factor)
    vectors_new, vector_moments_new = adam_update(
        vectors, vector_moments, vectors_grad, clip_factor
    )
    return (
        block_out,
        tokens_grad,
        qkv_grad,
        proj_grad,
        up_grad,
        down_grad,
        vectors_grad,
        qkv_new,
        proj_new,
        up_new,
        down_new,
        vectors_new,
        qkv_moments_new,
        proj_moments_new,
        up_moments_new,
        down_moments_new,
        vector_moments_new,
    )


def solution(mesh):
    placed = (
        P(("dp", "shard"), None),
        P(("dp", "shard"), None),
        P("dp", None),
        P("dp", "shard"),
        P("dp", "shard"),
        P("dp", "shard"),
        P("dp", "shard"),
        P(None, ("dp", "shard")),
        P(None, "dp", "shard"),
        P(None, "dp", "shard"),
        P(None, "dp", "shard"),
        P(None, "dp", "shard"),
        P(None, None, ("dp", "shard")),
    )
    return jax.shard_map(
        shards,
        mesh=mesh,
        in_specs=placed,
        out_specs=(
            P(("dp", "shard"), None),
            P(("dp", "shard"), None),
            P("dp", "shard"),
            P("dp", "shard"),
            P("dp", "shard"),
            P("dp", "shard"),
            P(None, ("dp", "shard")),
            P("dp", "shard"),
            P("dp", "shard"),
            P("dp", "shard"),
            P("dp", "shard"),
            P(None, ("dp", "shard")),
            P(None, "dp", "shard"),
            P(None, "dp", "shard"),
            P(None, "dp", "shard"),
            P(None, "dp", "shard"),
            P(None, None, ("dp", "shard")),
        ),
        check_vma=False,
    )
```
